32 devices in a mesh: lat: 8 (over z, y), lon: 4 (over x, core).
Axes of the slice: x: 2, y: 2, z: 4, core: 2. Of those that a mesh axis runs over, the one named last changes fastest.
Arguments:
- fields: bfloat16 [69, 128, 512], P(None, 'lat', 'lon'), may hold values from -6 to 6
- enc_kernel: bfloat16 [3, 3, 256, 69], replicated, may hold values from -0.25 to 0.25
- gen_kernel: bfloat16 [3, 3, 69, 256], replicated, may hold values from -0.125 to 0.125
- recon_grad: bfloat16 [69, 128, 512], P(None, 'lat', 'lon'), may hold values from -6 to 6
Outputs:
- rebuilt: bfloat16 [69, 128, 512], P(None, 'lat', 'lon')
- feat_grad: bfloat16 [256, 128, 512], P(None, 'lat', 'lon')
- enc_grad: float32 [3, 3, 256, 69], replicated
- gen_grad: float32 [3, 3, 69, 256], replicated
The draws below stay inside these ranges and needn't reach their ends.
All inputs are finite; a program needn't handle non-finite values.
Results may differ from the reference program's by a relative error of at most 0.0085.
Values may be sent and summed in bfloat16 or wider, within the bound.
A program may use at most 64 MiB of HBM per device.

```python
import jax
import jax.numpy as jnp
from jax import lax

CIN = 69
CH = 256
LAT = 128
LON = 512


def block_scale(key, extent, pieces, least, top_value):
    gain, own = 1.0, jax.random.fold_in(key, 6)
    for dim, parts in pieces:
        heights = jnp.exp(jax.random.uniform(jax.random.fold_in(own, dim), (parts,), jnp.float32, least / len(pieces), top_value / len(pieces)))
        gain = gain * jnp.repeat(heights, extent[dim] // parts).reshape([-1 if axis == dim else 1 for axis in range(len(extent))])
    return gain


def normal_values(key, extent, scale, most, cuts=(), dtype=jnp.bfloat16):
    gain = block_scale(key, extent, cuts, -0.22, 0.18) if cuts else 1.0
    drawn = jax.random.normal(key, extent, jnp.float32) * scale * gain
    return jnp.minimum(jnp.maximum(drawn, -most), most).astype(dtype)


def setup_inputs(seed: int = 0) -> dict:
    key_list = jax.random.split(jax.random.key(seed), 5)
    return {
        "fields": normal_values(key_list[0], (CIN, LAT, LON), 1.0, 6.0, ((1, 8), (2, 4))),
        "enc_kernel": normal_values(key_list[1], (3, 3, CH, CIN), (9 * CIN) ** -0.5, 0.25),
        "gen_kernel": normal_values(key_list[2], (3, 3, CIN, CH), (9 * CH) ** -0.5, 0.125),
        "recon_grad": normal_values(key_list[3], (CIN, LAT, LON), 1.0, 6.0, ((1, 8), (2, 4))),
    }


def pole_pad(source):
    lon_cells = source.shape[2]
    upper = jnp.roll(source[:, :1], lon_cells // 2, axis=2)
    lower = jnp.roll(source[:, -1:], lon_cells // 2, axis=2)
    stacked = jnp.concatenate([upper, source, lower], axis=1)
    return jnp.concatenate([stacked[:, :, -1:], stacked, stacked[:, :, :1]], axis=2)

def convolve(padded, kernel, height, width):
    running = jnp.zeros((kernel.shape[2], height * width), jnp.float32)
    for row_tap in range(3):
        for col_tap in range(3):
            section = padded[:, row_tap:row_tap + height, col_tap:col_tap + width].reshape(padded.shape[0], height * width)
            running = running + jnp.dot(kernel[row_tap, col_tap], section, preferred_element_type=jnp.float32)
    return running.reshape(kernel.shape[2], height, width)

def weight_grad(cotangent, padded, height, width):
    flat_cot = cotangent.reshape(cotangent.shape[0], height * width)
    taps = []
    for row_tap in range(3):
        row_list = []
        for col_tap in range(3):
            section = padded[:, row_tap:row_tap + height, col_tap:col_tap + width].reshape(padded.shape[0], height * width)
            row_list.append(lax.dot_general(flat_cot, section, (((1,), (1,)), ((), ())), preferred_element_type=jnp.float32))
        taps.append(jnp.stack(row_list))
    return jnp.stack(taps)

def adjoint_conv(cotangent, kernel, height, width):
    flat_cot = cotangent.reshape(cotangent.shape[0], height * width)
    spread = jnp.zeros((kernel.shape[3], height + 2, width + 2), jnp.float32)
    for row_tap in range(3):
        for col_tap in range(3):
            product = lax.dot_general(kernel[row_tap, col_tap], flat_cot, (((0,), (0,)), ((), ())), preferred_element_type=jnp.float32)
            spread = spread.at[:, row_tap:row_tap + height, col_tap:col_tap + width].add(product.reshape(kernel.shape[3], height, width))
    folded = spread[:, :, 1:-1]
    folded = folded.at[:, :, -1].add(spread[:, :, 0])
    folded = folded.at[:, :, 0].add(spread[:, :, -1])
    inner = folded[:, 1:-1]
    inner = inner.at[:, 0].add(jnp.roll(folded[:, 0], width // 2, axis=1))
    inner = inner.at[:, -1].add(jnp.roll(folded[:, -1], width // 2, axis=1))
    return inner

def reference(fields, enc_kernel, gen_kernel, recon_grad):
    height = fields.shape[1]
    width = fields.shape[2]
    padded_in = pole_pad(fields)
    pre_act = convolve(padded_in, enc_kernel, height, width)
    hidden = jax.nn.silu(pre_act).astype(jnp.bfloat16)
    padded_hid = pole_pad(hidden)
    rebuilt = convolve(padded_hid, gen_kernel, height, width).astype(jnp.bfloat16)
    feat_grad = adjoint_conv(recon_grad, gen_kernel, height, width).astype(jnp.bfloat16)
    logistic = jax.nn.sigmoid(pre_act)
    pre_grad = (feat_grad.astype(jnp.float32) * logistic * (1.0 + pre_act * (1.0 - logistic))).astype(jnp.bfloat16)
    norm_scale = 1.0 / jnp.sqrt(jnp.float32(LAT * LON))
    gen_grad = weight_grad(recon_grad, padded_hid, height, width) * norm_scale
    enc_grad = weight_grad(pre_grad, padded_in, height, width) * norm_scale
    return (rebuilt, feat_grad, enc_grad, gen_grad)
```

```python
import functools

import jax
import jax.numpy as jnp
from jax import lax
from jax.experimental import pallas as pl
from jax.experimental.pallas import tpu as pltpu
from jax.sharding import PartitionSpec as P

MESH = pl.DeviceIdType.MESH
SEND = jnp.float32


def extended(cells, sides, width, closed):
    for axis, dim in sides:
        count = lax.axis_size(axis)
        ends = count if closed else count - 1
        head = lax.slice_in_dim(cells, 0, width, axis=dim)
        tail = lax.slice_in_dim(cells, cells.shape[dim] - width, cells.shape[dim], axis=dim)
        cells = jnp.concatenate(
            [
                lax.ppermute(tail, axis, [(i, (i + 1) % count) for i in range(ends)]),
                cells,
                lax.ppermute(head, axis, [((i + 1) % count, i) for i in range(ends)]),
            ],
            axis=dim,
        )
    return cells


def from_behind(value, axis, steps):
    count = lax.axis_size(axis)
    pairs = [(source, (source + steps) % count) for source in range(count)]
    return lax.ppermute(value, axis, pairs)


def face_pad(source):
    lon_count = lax.axis_size("lon")
    widened = extended(source, (("lon", 2),), 1, True)
    edge_rows = jnp.concatenate([widened[:, :1], widened[:, -1:]], axis=1)
    pole_rows = from_behind(edge_rows, "lon", lon_count // 2)
    plain_pad = extended(widened, (("lat", 1),), 1, False)
    return (plain_pad, pole_rows)


def with_poles(plain_pad, pole_rows):
    lat_index = lax.axis_index("lat")
    lat_count = lax.axis_size("lat")
    upper = jnp.where(lat_index == 0, pole_rows[:, :1], plain_pad[:, :1])
    lower = jnp.where(lat_index == lat_count - 1, pole_rows[:, 1:], plain_pad[:, -1:])
    return jnp.concatenate([upper, plain_pad[:, 1:-1], lower], axis=1)


def reduce_kernel(lats, halves, a_ref, out_ref, from_pair, held_pair, from_lon, held_lon, from_lat, *sems):
    lat = lax.axis_index("lat")
    lon = lax.axis_index("lon")
    half = lax.div(lon, 2)
    core = lax.rem(lon, 2)
    other = 1 - core

    def lon_peer(step):
        return (lat, lax.rem(half + step, halves) * 2 + core)

    def lat_peer(step):
        return (lax.rem(lat + step, lats), lon)

    pair = (lat, half * 2 + other)
    barrier = pltpu.get_barrier_semaphore()
    peers = [pair]
    peers += [lon_peer(step) for step in range(1, halves)]
    peers += [lat_peer(step) for step in range(1, lats)]
    for peer in peers:
        pl.semaphore_signal(barrier, inc=1, device_id=peer, device_id_type=MESH)
    pl.semaphore_wait(barrier, len(peers))

    def send(src, dst, phase, slot, peer):
        copy = pltpu.make_async_remote_copy(
            src_ref=src,
            dst_ref=dst,
            send_sem=sems[2 * phase].at[slot],
            recv_sem=sems[2 * phase + 1].at[slot],
            device_id=peer,
            device_id_type=MESH,
        )
        copy.start()
        return copy

    send(a_ref.at[other], from_pair, 0, 0, pair).wait()
    held_pair[...] = (a_ref[core].astype(jnp.float32) + from_pair[...].astype(jnp.float32)).astype(
        held_pair.dtype
    )
    copies = []
    for step in range(1, halves):
        target = lax.rem(half + step, halves)
        copies.append(send(held_pair.at[target], from_lon.at[step - 1], 1, step - 1, lon_peer(step)))
    for copy in copies:
        copy.wait()
    total = held_pair[half].astype(jnp.float32)
    for step in range(1, halves):
        total = total + from_lon[step - 1].astype(jnp.float32)
    held_lon[...] = total.astype(held_lon.dtype)
    copies = []
    for step in range(1, lats):
        target = lax.rem(lat + step, lats)
        copies.append(send(held_lon.at[target], from_lat.at[step - 1], 2, step - 1, lat_peer(step)))
    for copy in copies:
        copy.wait()
    total = held_lon[lat].astype(jnp.float32)
    for step in range(1, lats):
        total = total + from_lat[step - 1].astype(jnp.float32)
    out_ref[core, half, lat] = total.astype(out_ref.dtype)
    mine = out_ref.at[core, half, lat]
    copies = [send(mine, mine, 3, step - 1, lat_peer(step)) for step in range(1, lats)]
    for copy in copies:
        copy.wait()
    mine = out_ref.at[core, half]
    copies = [send(mine, mine, 4, step - 1, lon_peer(step)) for step in range(1, halves)]
    for copy in copies:
        copy.wait()
    mine = out_ref.at[core]
    send(mine, mine, 5, 0, pair).wait()


def reduce_all(stacked):
    lats = lax.axis_size("lat")
    halves = lax.axis_size("lon") // 2
    rows, width = stacked.shape
    unit = 16
    piece = -(-rows // (2 * halves * lats * unit)) * unit
    padded = jnp.pad(stacked, ((0, 2 * halves * lats * piece - rows), (0, 0))).astype(SEND)
    parts = padded.reshape(2, halves, lats, piece, width)
    counts = [1, halves - 1, lats - 1, lats - 1, halves - 1, 1]
    out = pl.pallas_call(
        functools.partial(reduce_kernel, lats, halves),
        out_shape=jax.ShapeDtypeStruct(parts.shape, jnp.bfloat16),
        in_specs=[pl.BlockSpec(memory_space=pltpu.VMEM)],
        out_specs=pl.BlockSpec(memory_space=pltpu.VMEM),
        scratch_shapes=[
            pltpu.VMEM((halves, lats, piece, width), SEND),
            pltpu.VMEM((halves, lats, piece, width), SEND),
            pltpu.VMEM((halves - 1, lats, piece, width), SEND),
            pltpu.VMEM((lats, piece, width), SEND),
            pltpu.VMEM((lats - 1, piece, width), SEND),
        ]
        + [pltpu.SemaphoreType.DMA((count,)) for count in counts for _ in range(2)],
        compiler_params=pltpu.CompilerParams(collective_id=0, has_side_effects=True),
    )(parts)
    return out.reshape(-1, width)[:rows]


def columns(padded, height, width, flip):
    taps = []
    for row_tap in range(3):
        for col_tap in range(3):
            top = 2 - row_tap if flip else row_tap
            side = 2 - col_tap if flip else col_tap
            taps.append(padded[:, top : top + height, side : side + width])
    return jnp.stack(taps).reshape(9 * padded.shape[0], height * width)


def dot(left, right, dims):
    return lax.dot_general(left, right, (dims, ((), ())), preferred_element_type=jnp.float32)


def on_device(fields, enc_kernel, gen_kernel, recon_grad):
    in_count, height, width = fields.shape
    hid_count = enc_kernel.shape[2]
    deep = -(-in_count // 8) * 8
    extra = deep - in_count
    lat_index = lax.axis_index("lat")
    lat_count = lax.axis_size("lat")
    lon_count = lax.axis_size("lon")
    room = jnp.zeros((extra, height, width), fields.dtype)
    plain_pair, pole_pair = face_pad(jnp.concatenate([fields, room, recon_grad, room], axis=0))
    padded_in = with_poles(plain_pair[:deep], pole_pair[:deep])
    plain_cot = plain_pair[deep:]
    pole_cot = pole_pair[deep:]
    enc_flat = jnp.pad(enc_kernel, ((0, 0), (0, 0), (0, 0), (0, extra)))
    enc_flat = enc_flat.transpose(0, 1, 3, 2).reshape(9 * deep, hid_count)
    gen_taps = jnp.pad(gen_kernel, ((0, 0), (0, 0), (0, extra), (0, 0)))
    gen_flat = gen_taps.reshape(9 * deep, hid_count)

    in_cols = columns(padded_in, height, width, False)
    pre_act = dot(enc_flat, in_cols, ((0,), (0,)))
    hidden = jax.nn.silu(pre_act).astype(jnp.bfloat16)
    plain_hid, pole_hid = face_pad(hidden.reshape(hid_count, height, width))
    padded_hid = with_poles(plain_hid, pole_hid)

    cot_cols = columns(plain_cot, height, width, True)
    upper = jnp.where(lat_index == 0, pole_cot[:, 0], 0)
    lower = jnp.where(lat_index == lat_count - 1, pole_cot[:, 1], 0)
    upper_cols = jnp.concatenate([upper[:, 2 - b : 2 - b + width] for b in range(3)], axis=0)
    lower_cols = jnp.concatenate([lower[:, 2 - b : 2 - b + width] for b in range(3)], axis=0)
    band = 3 * deep
    feat_f32 = dot(gen_flat, cot_cols, ((0,), (0,)))
    upper_term = dot(gen_flat[:band], upper_cols, ((0,), (0,)))
    lower_term = dot(gen_flat[2 * band :], lower_cols, ((0,), (0,)))
    gap = jnp.zeros((hid_count, (height - 2) * width), jnp.float32)
    feat_f32 = feat_f32 + jnp.concatenate([upper_term, gap, lower_term], axis=1)
    feat_grad = feat_f32.astype(jnp.bfloat16)
    logistic = jax.nn.sigmoid(pre_act)
    pre_grad = (
        feat_grad.astype(jnp.float32) * logistic * (1.0 + pre_act * (1.0 - logistic))
    ).astype(jnp.bfloat16)

    gen_part = dot(cot_cols, hidden, ((1,), (1,)))
    gen_upper = dot(upper_cols, hidden[:, :width], ((1,), (1,)))
    gen_lower = dot(lower_cols, hidden[:, -width:], ((1,), (1,)))
    gen_part = gen_part + jnp.concatenate(
        [gen_upper, jnp.zeros((band, hid_count), jnp.float32), gen_lower], axis=0
    )
    enc_part = dot(in_cols, pre_grad, ((1,), (1,)))
    summed = reduce_all(jnp.concatenate([enc_part, gen_part], axis=0))
    norm_scale = 1.0 / jnp.sqrt(jnp.float32(height * lat_count * width * lon_count))
    summed = summed.reshape(2, 3, 3, deep, hid_count)[:, :, :, :in_count].astype(jnp.float32) * norm_scale

    spread = dot(gen_flat, padded_hid.reshape(hid_count, -1), ((1,), (0,)))
    spread = spread.reshape(3, 3, deep, height + 2, width + 2)
    rebuilt = None
    for row_tap in range(3):
        for col_tap in range(3):
            term = spread[
                row_tap, col_tap, :in_count, row_tap : row_tap + height, col_tap : col_tap + width
            ]
            rebuilt = term if rebuilt is None else rebuilt + term
    return (
        rebuilt.astype(jnp.bfloat16),
        feat_grad.reshape(hid_count, height, width),
        summed[0].transpose(0, 1, 3, 2),
        summed[1],
    )


def solution(mesh):
    return jax.shard_map(
        on_device,
        mesh=mesh,
        in_specs=(P(None, "lat", "lon"), P(), P(), P(None, "lat", "lon")),
        out_specs=(P(None, "lat", "lon"), P(None, "lat", "lon"), P(), P()),
        check_vma=False,
    )
```

```python
import functools

import jax
import jax.numpy as jnp
from jax import lax
from jax.experimental import pallas as pl
from jax.experimental.pallas import tpu as pltpu
from jax.sharding import PartitionSpec as P

MESH = pl.DeviceIdType.MESH
SEND = jnp.float32
F32 = jnp.float32
BF16 = jnp.bfloat16


def dot(left, right, dims):
    return lax.dot_general(left, right, (dims, ((), ())), preferred_element_type=F32)


def shifted(value, amount):
    return pltpu.roll(value, amount, 1)


def pack_columns(load, out_ref, count, group, height, width):
    lane = lax.broadcasted_iota(jnp.int32, (group, width), 1)
    for start in range(0, count, group):
        first = jnp.zeros((group, width), F32)
        last = jnp.zeros((group, width), F32)
        for row in range(height):
            cells = load(row, start, group).astype(F32)
            first = jnp.where(lane == row, shifted(cells, row) if row else cells, first)
            last = jnp.where(lane == row, shifted(cells, row + 1), last)
        out_ref[0, start : start + group] = first.astype(BF16)
        out_ref[1, start : start + group] = last.astype(BF16)


def widen_row(load, halo_ref, row, start, group, width):
    lane = lax.broadcasted_iota(jnp.int32, (group, width), 1)
    cells = load(row, start, group)
    wide = cells.astype(F32)
    left = shifted(halo_ref[0, start : start + group].astype(F32), lax.rem(width - row, width))
    right = shifted(halo_ref[1, start : start + group].astype(F32), width - 1 - row)
    before = jnp.where(lane == 0, left, shifted(wide, 1)).astype(BF16)
    after = jnp.where(lane == width - 1, right, shifted(wide, width - 1)).astype(BF16)
    return before, cells, after


def layer_kernel(
    lats, halves, deep, wide_deep, in_ref, we_ref, wf_ref, wr_ref, reb_ref, feat_ref, grad_ref,
    xg, hs, hrow, packed, arrived, hpacked, harrived, accx, accg, parts,
    from_pair, held_pair, from_lon, held_lon, from_lat, *sems,
):
    height, both, width = in_ref.shape
    hid = hrow.shape[1]
    lons = 2 * halves
    band = 3 * wide_deep
    lat = lax.axis_index("lat")
    lon = lax.axis_index("lon")
    half = lax.div(lon, 2)
    core = lax.rem(lon, 2)
    other = 1 - core
    below_top = lax.div(lat + lats - 1, lats)
    above_end = lax.div(2 * lats - 2 - lat, lats)

    def lon_peer(step):
        return (lat, lax.rem(half + step, halves) * 2 + core)

    def lat_peer(step):
        return (lax.rem(lat + step, lats), lon)

    pair = (lat, half * 2 + other)
    outer = (lat, lax.rem(lon + lons + 2 * core - 1, lons))
    west = (lat, lax.rem(lon + lons - 1, lons))
    east = (lat, lax.rem(lon + 1, lons))
    north = (lat - below_top, lax.rem(lon + (1 - below_top) * halves, lons))
    south = (lat + above_end, lax.rem(lon + (1 - above_end) * halves, lons))

    barrier = pltpu.get_barrier_semaphore()
    peers = [pair, outer]
    peers += [lon_peer(step) for step in range(1, halves)]
    peers += [lat_peer(step) for step in range(1, lats)]
    for peer in peers:
        pl.semaphore_signal(barrier, inc=1, device_id=peer, device_id_type=MESH)
    pl.semaphore_wait(barrier, len(peers))

    def send(src, dst, phase, send_slot, recv_slot, peer):
        copy = pltpu.make_async_remote_copy(
            src_ref=src,
            dst_ref=dst,
            send_sem=sems[2 * phase].at[send_slot],
            recv_sem=sems[2 * phase + 1].at[recv_slot],
            device_id=peer,
            device_id_type=MESH,
        )
        copy.start()
        return copy

    def swap_columns(source, target, phase):
        return [
            send(source.at[1], target.at[0], phase, 0, 0, east),
            send(source.at[0], target.at[1], phase, 1, 1, west),
        ]

    def swap_rows(rows, phase):
        return [
            send(rows.at[1], rows.at[below_top * (height + 1)], phase, 0, below_top, north),
            send(rows.at[height], rows.at[(1 - above_end) * (height + 1)], phase, 1, 1 - above_end, south),
        ]

    def wait_rows(copies, rows, phase):
        for copy in copies:
            copy.wait_send()
        for slot in range(2):
            edge = rows.at[slot * (height + 1)]
            pltpu.make_async_copy(edge, edge, sems[2 * phase + 1].at[slot]).wait()

    def load_in(row, start, group):
        return in_ref[row, start : start + group]

    pack_columns(load_in, packed, both, both // 2, height, width)
    copies = swap_columns(packed, arrived, 6)
    accx[...] = jnp.zeros_like(accx)
    accg[...] = jnp.zeros_like(accg)
    for copy in copies:
        copy.wait()

    def widen_in(row):
        before, cells, after = widen_row(load_in, arrived, row, 0, wide_deep, width)
        for place, value in enumerate((before, cells, after)):
            xg[row + 1, place * wide_deep : (place + 1) * wide_deep] = value
        before, cells, after = widen_row(load_in, arrived, row, wide_deep, wide_deep, width)
        for place, value in enumerate((after, cells, before)):
            xg[row + 1, band + place * wide_deep : band + (place + 1) * wide_deep] = value

    widen_in(0)
    widen_in(height - 1)
    copies = swap_rows(xg, 7)

    @pl.loop(1, height - 1)
    def _(row):
        widen_in(row)

    def window(ref, row, start, count):
        tall = 3 * count
        return jnp.concatenate(
            [
                ref[pl.ds(row, 3), start : start + count].reshape(tall, width),
                ref[pl.ds(row + 1, 3), start : start + count].reshape(tall, width),
            ],
            axis=1,
        )

    def cells_step(row, extra):
        in_cols = window(xg, row, 0, band)
        cot_cols = window(xg, row, band, band)
        pre_act = dot(we_ref[...], in_cols, ((1,), (0,)))
        logistic = 1.0 / (1.0 + jnp.exp(-pre_act))
        hidden = (pre_act * logistic).astype(BF16)
        hrow[row] = hidden[:, :width]
        hrow[row + 1] = hidden[:, width:]
        feat = dot(wf_ref[...], cot_cols, ((1,), (0,)))
        if extra is not None:
            feat = feat + extra
        feat = feat.astype(BF16)
        feat_ref[row] = feat[:, :width]
        feat_ref[row + 1] = feat[:, width:]
        pre_grad = (
            feat.astype(F32) * logistic * (1.0 + pre_act * (1.0 - logistic))
        ).astype(BF16)
        accg[...] += dot(cot_cols, hidden, ((1,), (1,)))
        accx[...] += dot(in_cols, pre_grad, ((1,), (1,)))

    @pl.loop(1, height // 2 - 1)
    def _(step):
        cells_step(step * 2, None)

    wait_rows(copies, xg, 7)
    open_gap = jnp.zeros((hid, width), F32)
    for slot, inside, start, row in ((0, below_top, 2 * band, 0), (1, above_end, 0, height - 2)):
        edge = xg[slot * (height + 1), band:]
        at_pole = jnp.where(inside == 0, edge, jnp.zeros_like(edge))
        xg[slot * (height + 1), band:] = jnp.where(inside == 0, jnp.zeros_like(edge), edge)
        term = dot(wf_ref[:, start : start + band], at_pole, ((1,), (0,)))
        both_terms = [term, open_gap] if slot == 0 else [open_gap, term]
        cells_step(row, jnp.concatenate(both_terms, axis=1))
        accg[start : start + band] += dot(at_pole, hrow[row + slot], ((1,), (1,)))

    def load_hid(row, start, group):
        return hrow[row, start : start + group]

    for tap in range(9):
        row_tap, col_tap = divmod(tap, 3)
        source = (2 - row_tap) * 3 + col_tap
        parts[tap * deep : (tap + 1) * deep] = accx[
            tap * wide_deep : tap * wide_deep + deep
        ].astype(SEND)
        parts[(9 + tap) * deep : (10 + tap) * deep] = accg[
            source * wide_deep : source * wide_deep + deep
        ].astype(SEND)
    used = 18 * deep
    if parts.shape[0] > used:
        parts[used:] = jnp.zeros((parts.shape[0] - used, hid), SEND)

    half_rows = parts.shape[0] // 2
    lon_rows = half_rows // halves
    lat_rows = lon_rows // lats

    def at(ref, index, count):
        return ref.at[pl.ds(pl.multiple_of(index * count, 16), count)]

    pair_copy = send(at(parts, other, half_rows), from_pair, 0, 0, 0, pair)
    pack_columns(load_hid, hpacked, hid, 64, height, width)
    column_copies = swap_columns(hpacked, harrived, 8)
    pair_copy.wait()
    held_pair[...] = (at(parts, core, half_rows)[...].astype(F32) + from_pair[...].astype(F32)).astype(SEND)
    lon_copies = []
    for step in range(1, halves):
        target = lax.rem(half + step, halves)
        lon_copies.append(
            send(at(held_pair, target, lon_rows), from_lon.at[step - 1], 1, step - 1, step - 1, lon_peer(step))
        )
    for copy in column_copies:
        copy.wait()

    def widen_hid(row):
        for start in range(0, hid, 64):
            parts_row = widen_row(load_hid, harrived, row, start, 64, width)
            for place, value in enumerate(parts_row):
                hs[row + 1, place * hid + start : place * hid + start + 64] = value

    widen_hid(0)
    widen_hid(height - 1)
    row_copies = swap_rows(hs, 9)

    @pl.loop(1, height - 1)
    def _(row):
        widen_hid(row)

    for copy in lon_copies:
        copy.wait()
    total = at(held_pair, half, lon_rows)[...].astype(F32)
    for step in range(1, halves):
        total = total + from_lon[step - 1].astype(F32)
    held_lon[...] = total.astype(SEND)
    lat_copies = []
    for step in range(1, lats):
        target = lax.rem(lat + step, lats)
        lat_copies.append(
            send(at(held_lon, target, lat_rows), from_lat.at[step - 1], 2, step - 1, step - 1, lat_peer(step))
        )

    def rebuild(row):
        value = dot(wr_ref[...], window(hs, row, 0, 3 * hid), ((1,), (0,))).astype(BF16)
        reb_ref[row] = value[:, :width]
        reb_ref[row + 1] = value[:, width:]

    @pl.loop(1, height // 2 - 1)
    def _(step):
        rebuild(step * 2)

    for copy in lat_copies:
        copy.wait()
    total = at(held_lon, lat, lat_rows)[...].astype(F32)
    for step in range(1, lats):
        total = total + from_lat[step - 1].astype(F32)
    place = (core * halves + half) * lats + lat
    mine = at(grad_ref, place, lat_rows)
    mine[...] = total.astype(grad_ref.dtype)
    copies = [send(mine, mine, 3, step - 1, step - 1, lat_peer(step)) for step in range(1, lats)]
    wait_rows(row_copies, hs, 9)
    rebuild(0)
    rebuild(height - 2)
    for copy in copies:
        copy.wait()
    mine = at(grad_ref, core * halves + half, lon_rows)
    copies = [send(mine, mine, 4, step - 1, step - 1, lon_peer(step)) for step in range(1, halves)]
    for copy in copies:
        copy.wait()
    mine = at(grad_ref, core, half_rows)
    send(mine, mine, 5, 0, 0, pair).wait()


def on_device(fields, enc_kernel, gen_kernel, recon_grad):
    in_count, height, width = fields.shape
    hid = enc_kernel.shape[2]
    deep = -(-in_count // 8) * 8
    wide_deep = -(-in_count // 16) * 16
    extra = wide_deep - in_count
    lats = lax.axis_size("lat")
    lons = lax.axis_size("lon")
    halves = lons // 2
    room = ((0, 0), (0, extra), (0, 0))
    stacked = jnp.concatenate(
        [
            jnp.pad(fields.transpose(1, 0, 2), room),
            jnp.pad(recon_grad.transpose(1, 0, 2), room),
        ],
        axis=1,
    )
    band = 3 * wide_deep
    enc_flat = jnp.pad(enc_kernel, ((0, 0), (0, 0), (0, 0), (0, extra)))
    enc_flat = enc_flat.transpose(2, 0, 1, 3).reshape(hid, 3 * band)
    gen_taps = jnp.pad(gen_kernel, ((0, 0), (0, 0), (0, extra), (0, 0)))
    back_flat = gen_taps[::-1].transpose(3, 0, 1, 2).reshape(hid, 3 * band)
    gen_flat = gen_taps.transpose(2, 0, 1, 3).reshape(wide_deep, 9 * hid)
    pieces = lons * lats
    lat_rows = -(-18 * deep // (pieces * 16)) * 16
    lon_rows = lats * lat_rows
    half_rows = halves * lon_rows
    counts = [1, halves - 1, lats - 1, lats - 1, halves - 1, 1, 2, 2, 2, 2]
    rebuilt, feat, summed = pl.pallas_call(
        functools.partial(layer_kernel, lats, halves, deep, wide_deep),
        out_shape=[
            jax.ShapeDtypeStruct((height, wide_deep, width), BF16),
            jax.ShapeDtypeStruct((height, hid, width), BF16),
            jax.ShapeDtypeStruct((2 * half_rows, hid), BF16),
        ],
        in_specs=[pl.BlockSpec(memory_space=pltpu.VMEM)] * 4,
        out_specs=[pl.BlockSpec(memory_space=pltpu.VMEM)] * 3,
        scratch_shapes=[
            pltpu.VMEM((height + 2, 2 * band, width), BF16),
            pltpu.VMEM((height + 2, 3 * hid, width), BF16),
            pltpu.VMEM((height, hid, width), BF16),
            pltpu.VMEM((2, 2 * wide_deep, width), BF16),
            pltpu.VMEM((2, 2 * wide_deep, width), BF16),
            pltpu.VMEM((2, hid, width), BF16),
            pltpu.VMEM((2, hid, width), BF16),
            pltpu.VMEM((3 * band, hid), F32),
            pltpu.VMEM((3 * band, hid), F32),
            pltpu.VMEM((2 * half_rows, hid), SEND),
            pltpu.VMEM((half_rows, hid), SEND),
            pltpu.VMEM((half_rows, hid), SEND),
            pltpu.VMEM((halves - 1, lon_rows, hid), SEND),
            pltpu.VMEM((lon_rows, hid), SEND),
            pltpu.VMEM((lats - 1, lat_rows, hid), SEND),
        ]
        + [pltpu.SemaphoreType.DMA((count,)) for count in counts for _ in range(2)],
        compiler_params=pltpu.CompilerParams(
            collective_id=0, has_side_effects=True, vmem_limit_bytes=48 << 20
        ),
    )(stacked, enc_flat, back_flat, gen_flat)
    norm_scale = 1.0 / jnp.sqrt(F32(height * lats * width * lons))
    grads = summed[: 18 * deep].reshape(2, 3, 3, deep, hid)[:, :, :, :in_count].astype(F32) * norm_scale
    return (
        rebuilt[:, :in_count].transpose(1, 0, 2),
        feat.transpose(1, 0, 2),
        grads[0].transpose(0, 1, 3, 2),
        grads[1],
    )


def solution(mesh):
    return jax.shard_map(
        on_device,
        mesh=mesh,
        in_specs=(P(None, "lat", "lon"), P(), P(), P(None, "lat", "lon")),
        out_specs=(P(None, "lat", "lon"), P(None, "lat", "lon"), P(), P()),
        check_vma=False,
    )
```

```python
import functools

import jax
import jax.numpy as jnp
from jax import lax
from jax.experimental import pallas as pl
from jax.experimental.pallas import tpu as pltpu
from jax.sharding import PartitionSpec as P

MESH = pl.DeviceIdType.MESH
LINK = jnp.bfloat16
F32 = jnp.float32
BF16 = jnp.bfloat16


def dot(left, right, dims):
    return lax.dot_general(left, right, (dims, ((), ())), preferred_element_type=F32)


def shifted(value, amount):
    return pltpu.roll(value, amount, 1)


def pack_columns(load, out_ref, count, group, tall, width):
    lane = lax.broadcasted_iota(jnp.int32, (group, width), 1)
    for start in range(0, count, group):
        first = jnp.zeros((group, width), F32)
        last = jnp.zeros((group, width), F32)
        for row in range(tall):
            cells = load(row, start, group).astype(F32)
            first = jnp.where(lane == row, shifted(cells, row) if row else cells, first)
            last = jnp.where(lane == row, shifted(cells, row + 1), last)
        out_ref[0, start : start + group] = first.astype(BF16)
        out_ref[1, start : start + group] = last.astype(BF16)


def widen_row(load, halo_ref, row, start, group, width):
    lane = lax.broadcasted_iota(jnp.int32, (group, width), 1)
    cells = load(row, start, group)
    wide = cells.astype(F32)
    left = shifted(halo_ref[0, start : start + group].astype(F32), lax.rem(width - row, width))
    right = shifted(halo_ref[1, start : start + group].astype(F32), width - 1 - row)
    before = jnp.where(lane == 0, left, shifted(wide, 1)).astype(BF16)
    after = jnp.where(lane == width - 1, right, shifted(wide, width - 1)).astype(BF16)
    return before, cells, after


def padded_loader(inner, halo, height):
    def load(row, start, group):
        if isinstance(row, int) and row in (0, height + 1):
            return halo[min(row, 1), start : start + group]
        return inner[row - 1, start : start + group]

    return load


def layer_kernel(
    lats, halves, deep, wide_deep, in_ref, we_ref, wf_ref, wr_ref, reb_ref, feat_ref, grad_ref,
    xg, hs, hrow, pre, inhalo, hidhalo, packed, arrived, hpacked, harrived, accx, accg, parts,
    from_pair, lon_out, from_lon, lat_out, from_lat, *sems,
):
    height, both, width = in_ref.shape
    hid = hrow.shape[1]
    lons = 2 * halves
    band = 3 * wide_deep
    lat = lax.axis_index("lat")
    lon = lax.axis_index("lon")
    half = lax.div(lon, 2)
    core = lax.rem(lon, 2)
    other = 1 - core
    below_top = lax.div(lat + lats - 1, lats)
    above_end = lax.div(2 * lats - 2 - lat, lats)

    def lon_peer(step):
        return (lat, lax.rem(half + step, halves) * 2 + core)

    def lat_peer(step):
        return (lax.rem(lat + step, lats), lon)

    pair = (lat, half * 2 + other)
    outer = (lat, lax.rem(lon + lons + 2 * core - 1, lons))
    west = (lat, lax.rem(lon + lons - 1, lons))
    east = (lat, lax.rem(lon + 1, lons))
    north = (lat - below_top, lax.rem(lon + (1 - below_top) * halves, lons))
    south = (lat + above_end, lax.rem(lon + (1 - above_end) * halves, lons))

    barrier = pltpu.get_barrier_semaphore()
    peers = [pair, outer]
    peers += [lon_peer(step) for step in range(1, halves)]
    peers += [lat_peer(step) for step in range(1, lats)]
    for peer in peers:
        pl.semaphore_signal(barrier, inc=1, device_id=peer, device_id_type=MESH)

    def send(src, dst, phase, send_slot, recv_slot, peer):
        copy = pltpu.make_async_remote_copy(
            src_ref=src,
            dst_ref=dst,
            send_sem=sems[2 * phase].at[send_slot],
            recv_sem=sems[2 * phase + 1].at[recv_slot],
            device_id=peer,
            device_id_type=MESH,
        )
        copy.start()
        return copy

    def swap_columns(source, target, phase):
        return [
            send(source.at[1], target.at[0], phase, 0, 0, east),
            send(source.at[0], target.at[1], phase, 1, 1, west),
        ]

    def swap_rows(rows, halo, phase):
        return [
            send(rows.at[0], halo.at[below_top], phase, 0, below_top, north),
            send(rows.at[height - 1], halo.at[1 - above_end], phase, 1, 1 - above_end, south),
        ]

    def wait_rows(copies, halo, phase):
        for copy in copies:
            copy.wait_send()
        for slot in range(2):
            edge = halo.at[slot]
            pltpu.make_async_copy(edge, edge, sems[2 * phase + 1].at[slot]).wait()

    load_in = padded_loader(in_ref, inhalo, height)
    load_hid = padded_loader(hrow, hidhalo, height)
    pl.semaphore_wait(barrier, len(peers))
    copies = swap_rows(in_ref, inhalo, 13)
    accx[...] = jnp.zeros_like(accx)
    accg[...] = jnp.zeros_like(accg)
    wait_rows(copies, inhalo, 13)
    pack_columns(load_in, packed, both, both // 2, height + 2, width)
    copies = swap_columns(packed, arrived, 12)
    for copy in copies:
        copy.wait()

    def widen_in(row):
        before, cells, after = widen_row(load_in, arrived, row, 0, wide_deep, width)
        for place, value in enumerate((before, cells, after)):
            xg[row, place * wide_deep : (place + 1) * wide_deep] = value
        before, cells, after = widen_row(load_in, arrived, row, wide_deep, wide_deep, width)
        for place, value in enumerate((after, cells, before)):
            xg[row, band + place * wide_deep : band + (place + 1) * wide_deep] = value

    widen_in(0)
    widen_in(height + 1)

    @pl.loop(1, height + 1)
    def _(row):
        widen_in(row)

    def window(ref, row, start, count):
        return jnp.concatenate(
            [
                ref[pl.ds(row + place, 3), start : start + count].reshape(3 * count, width)
                for place in range(rows)
            ],
            axis=1,
        )

    def first_step(step):
        row = step * rows
        in_cols = window(xg, row, 0, band)
        cot_cols = window(xg, row, band, band)
        pre_act = dot(we_ref[...], in_cols, ((1,), (0,)))
        pre[step] = pre_act
        hidden = (pre_act * (1.0 / (1.0 + jnp.exp(-pre_act)))).astype(BF16)
        for place in range(rows):
            hrow[row + place] = hidden[:, place * width : (place + 1) * width]
        accg[...] += dot(cot_cols, hidden, ((1,), (1,)))

    def second_step(step, extra):
        row = step * rows
        in_cols = window(xg, row, 0, band)
        cot_cols = window(xg, row, band, band)
        pre_act = pre[step]
        logistic = 1.0 / (1.0 + jnp.exp(-pre_act))
        feat = dot(wf_ref[...], cot_cols, ((1,), (0,)))
        if extra is not None:
            feat = feat + extra
        feat = feat.astype(BF16)
        for place in range(rows):
            feat_ref[row + place] = feat[:, place * width : (place + 1) * width]
        pre_grad = (
            feat.astype(F32) * logistic * (1.0 + pre_act * (1.0 - logistic))
        ).astype(BF16)
        accx[...] += dot(in_cols, pre_grad, ((1,), (1,)))

    rows = 4
    steps = height // rows
    ends = ((0, below_top, 2 * band, 0), (1, above_end, 0, height - 1))
    at_poles = []
    for slot, inside, start, row in ends:
        edge = xg[slot * (height + 1), band:]
        at_poles.append(jnp.where(inside == 0, edge, jnp.zeros_like(edge)))
        xg[slot * (height + 1), band:] = jnp.where(inside == 0, jnp.zeros_like(edge), edge)
    first_step(0)
    first_step(steps - 1)
    row_copies = swap_rows(hrow, hidhalo, 15)

    @pl.loop(1, steps - 1)
    def _(step):
        first_step(step)

    for slot, inside, start, row in ends:
        accg[start : start + band] += dot(at_poles[slot], hrow[row], ((1,), (1,)))

    lane = hid // 2
    lane_rows = parts.shape[2]
    lon_rows = lane_rows // halves
    lat_rows = lon_rows // lats

    def fill(stream, acc, backward):
        for tap in range(9):
            row_tap, col_tap = divmod(tap, 3)
            source = ((2 - row_tap) * 3 + col_tap if backward else tap) * wide_deep
            for side in range(2):
                parts[stream, side, tap * deep : (tap + 1) * deep] = acc[
                    source : source + deep, side * lane : (side + 1) * lane
                ]
        used = 9 * deep
        if lane_rows > used:
            for side in range(2):
                parts[stream, side, used:] = jnp.zeros((lane_rows - used, lane), F32)

    def piece(index, count):
        return pl.ds(pl.multiple_of(index * count, 16), count)

    order = sorted(range(1, lats), key=lambda step: abs(2 * step - lats))

    def start_pair(stream):
        copies = {}
        for step in list(range(1, halves)) + [0]:
            part = piece(lax.rem(half + step, halves), lon_rows)
            copies[step] = send(
                parts.at[stream, other, part], from_pair.at[stream, part], stream * 6, step, step, pair
            )
        return copies

    def start_lon(stream, copies):
        onward = {}
        for step in range(1, halves):
            copies[step].wait()
            target = lax.rem(half + step, halves)
            part = piece(target, lon_rows)
            lon_out[stream, part] = (parts[stream, core, part] + from_pair[stream, part]).astype(LINK)
            for turn in order + [0]:
                there = lax.rem(lat + turn, lats)
                onward[step, turn] = send(
                    lon_out.at[stream, piece(target * lats + there, lat_rows)],
                    from_lon.at[stream, step - 1, piece(there, lat_rows)],
                    stream * 6 + 1, (step - 1) * lats + turn, (step - 1) * lats + turn, lon_peer(step),
                )
        copies[0].wait()
        return onward

    def lon_total(stream, copies, turn):
        there = lax.rem(lat + turn, lats)
        part = piece(half * lats + there, lat_rows)
        total = parts[stream, core, part] + from_pair[stream, part]
        for step in range(1, halves):
            copies[step, turn].wait()
            total = total + from_lon[stream, step - 1, piece(there, lat_rows)].astype(F32)
        return total

    def start_lat(stream, copies):
        onward = []
        for turn in order:
            there = piece(lax.rem(lat + turn, lats), lat_rows)
            lat_out[stream, there] = lon_total(stream, copies, turn).astype(LINK)
            onward.append(
                send(
                    lat_out.at[stream, there], from_lat.at[stream, turn - 1],
                    stream * 6 + 2, turn - 1, turn - 1, lat_peer(turn),
                )
            )
        return onward, lon_total(stream, copies, 0)

    def spread(stream, turn, lon_copies, pair_copies):
        there = lax.rem(lat + lats - turn, lats)
        mine = grad_ref.at[stream, core, piece(half * lats + there, lat_rows)]
        for step in range(1, halves):
            slot = (step - 1) * lats + turn
            lon_copies[step, turn] = send(mine, mine, stream * 6 + 4, slot, slot, lon_peer(step))
        pair_copies.append(send(mine, mine, stream * 6 + 5, turn, turn, pair))

    def start_lat_gather(stream, started):
        copies, total = started
        for turn, copy in zip(order, copies):
            copy.wait()
            total = total + from_lat[stream, turn - 1].astype(F32)
        place = piece(half * lats + lat, lat_rows)
        grad_ref[stream, core, place] = total.astype(grad_ref.dtype)
        mine = grad_ref.at[stream, core, place]
        copies = [
            send(mine, mine, stream * 6 + 3, turn - 1, turn - 1, lat_peer(turn)) for turn in order
        ]
        lon_copies, pair_copies = {}, []
        spread(stream, 0, lon_copies, pair_copies)
        return copies, lon_copies, pair_copies

    def start_spread(stream, started):
        copies, lon_copies, pair_copies = started
        for turn, copy in reversed(list(zip(order, copies))):
            copy.wait()
            spread(stream, turn, lon_copies, pair_copies)
        return lon_copies, pair_copies

    def start_pair_gather(stream, started):
        lon_copies, pair_copies = started
        for turn in [0] + order[::-1]:
            for step in range(1, halves):
                lon_copies[step, turn].wait()
                source = lax.rem(half + halves - step, halves)
                there = lax.rem(lat + lats - turn, lats)
                mine = grad_ref.at[stream, core, piece(source * lats + there, lat_rows)]
                slot = step * lats + turn
                pair_copies.append(send(mine, mine, stream * 6 + 5, slot, slot, pair))
        return pair_copies

    fill(0, accg, True)
    gen_copies = start_pair(0)
    wait_rows(row_copies, hidhalo, 15)
    pack_columns(load_hid, hpacked, hid, 64, height + 2, width)
    column_copies = swap_columns(hpacked, harrived, 14)
    gen_copies = start_lon(0, gen_copies)

    @pl.loop(1, steps - 1)
    def _(step):
        second_step(step, None)

    gen_copies = start_lat(0, gen_copies)
    open_gap = jnp.zeros((hid, (rows - 1) * width), F32)
    for slot, inside, start, row in ends:
        term = dot(wf_ref[:, start : start + band], at_poles[slot], ((1,), (0,)))
        both_terms = [term, open_gap] if slot == 0 else [open_gap, term]
        second_step(row // rows, jnp.concatenate(both_terms, axis=1))
    fill(1, accx, False)
    enc_copies = start_pair(1)
    for copy in column_copies:
        copy.wait()
    gen_copies = start_lat_gather(0, gen_copies)
    enc_copies = start_lon(1, enc_copies)

    def widen_hid(row):
        for start in range(0, hid, 64):
            parts_row = widen_row(load_hid, harrived, row, start, 64, width)
            for place, value in enumerate(parts_row):
                hs[row, place * hid + start : place * hid + start + 64] = value

    widen_hid(0)
    widen_hid(height + 1)

    @pl.loop(1, height // 2)
    def _(row):
        widen_hid(row)

    enc_copies = start_lat(1, enc_copies)

    @pl.loop(height // 2, height + 1)
    def _(row):
        widen_hid(row)

    gen_copies = start_spread(0, gen_copies)
    enc_copies = start_lat_gather(1, enc_copies)

    @pl.loop(0, steps)
    def _(step):
        value = dot(wr_ref[...], window(hs, step * rows, 0, 3 * hid), ((1,), (0,))).astype(BF16)
        for place in range(rows):
            reb_ref[step * rows + place] = value[:, place * width : (place + 1) * width]

    gen_copies = start_pair_gather(0, gen_copies)
    enc_copies = start_spread(1, enc_copies)
    enc_copies = start_pair_gather(1, enc_copies)
    for copy in gen_copies + enc_copies:
        copy.wait()


def on_device(fields, enc_kernel, gen_kernel, recon_grad):
    in_count, height, width = fields.shape
    hid = enc_kernel.shape[2]
    deep = -(-in_count // 8) * 8
    wide_deep = -(-in_count // 16) * 16
    extra = wide_deep - in_count
    lats = lax.axis_size("lat")
    lons = lax.axis_size("lon")
    halves = lons // 2
    room = ((0, 0), (0, extra), (0, 0))
    stacked = jnp.concatenate(
        [
            jnp.pad(fields.transpose(1, 0, 2), room),
            jnp.pad(recon_grad.transpose(1, 0, 2), room),
        ],
        axis=1,
    )
    band = 3 * wide_deep
    enc_flat = jnp.pad(enc_kernel, ((0, 0), (0, 0), (0, 0), (0, extra)))
    enc_flat = enc_flat.transpose(2, 0, 1, 3).reshape(hid, 3 * band)
    gen_taps = jnp.pad(gen_kernel, ((0, 0), (0, 0), (0, extra), (0, 0)))
    back_flat = gen_taps[::-1].transpose(3, 0, 1, 2).reshape(hid, 3 * band)
    gen_flat = gen_taps.transpose(2, 0, 1, 3).reshape(wide_deep, 9 * hid)
    lane = hid // 2
    lat_rows = -(-9 * deep // (halves * lats * 16)) * 16
    lon_rows = lats * lat_rows
    lane_rows = halves * lon_rows
    hops = (halves - 1) * lats
    counts = [halves, hops, lats - 1, lats - 1, hops, halves * lats] * 2 + [2] * 4
    rebuilt, feat, summed = pl.pallas_call(
        functools.partial(layer_kernel, lats, halves, deep, wide_deep),
        out_shape=[
            jax.ShapeDtypeStruct((height, wide_deep, width), BF16),
            jax.ShapeDtypeStruct((height, hid, width), BF16),
            jax.ShapeDtypeStruct((2, 2, lane_rows, lane), BF16),
        ],
        in_specs=[pl.BlockSpec(memory_space=pltpu.VMEM)] * 4,
        out_specs=[pl.BlockSpec(memory_space=pltpu.VMEM)] * 3,
        scratch_shapes=[
            pltpu.VMEM((height + 2, 2 * band, width), BF16),
            pltpu.VMEM((height + 2, 3 * hid, width), BF16),
            pltpu.VMEM((height, hid, width), BF16),
            pltpu.VMEM((height // 4, hid, 4 * width), F32),
            pltpu.VMEM((2, 2 * wide_deep, width), BF16),
            pltpu.VMEM((2, hid, width), BF16),
            pltpu.VMEM((2, 2 * wide_deep, width), BF16),
            pltpu.VMEM((2, 2 * wide_deep, width), BF16),
            pltpu.VMEM((2, hid, width), BF16),
            pltpu.VMEM((2, hid, width), BF16),
            pltpu.VMEM((3 * band, hid), F32),
            pltpu.VMEM((3 * band, hid), F32),
            pltpu.VMEM((2, 2, lane_rows, lane), F32),
            pltpu.VMEM((2, lane_rows, lane), F32),
            pltpu.VMEM((2, lane_rows, lane), LINK),
            pltpu.VMEM((2, halves - 1, lon_rows, lane), LINK),
            pltpu.VMEM((2, lon_rows, lane), LINK),
            pltpu.VMEM((2, lats - 1, lat_rows, lane), LINK),
        ]
        + [pltpu.SemaphoreType.DMA((count,)) for count in counts for _ in range(2)],
        compiler_params=pltpu.CompilerParams(
            collective_id=0, has_side_effects=True, vmem_limit_bytes=48 << 20
        ),
    )(stacked, enc_flat, back_flat, gen_flat)
    norm_scale = 1.0 / jnp.sqrt(F32(height * lats * width * lons))
    grads = jnp.concatenate([summed[:, 0, : 9 * deep], summed[:, 1, : 9 * deep]], axis=2)
    grads = grads.reshape(2, 3, 3, deep, hid)[:, :, :, :in_count].astype(F32) * norm_scale
    return (
        rebuilt[:, :in_count].transpose(1, 0, 2),
        feat.transpose(1, 0, 2),
        grads[1].transpose(0, 1, 3, 2),
        grads[0],
    )


def solution(mesh):
    return jax.shard_map(
        on_device,
        mesh=mesh,
        in_specs=(P(None, "lat", "lon"), P(), P(), P(None, "lat", "lon")),
        out_specs=(P(None, "lat", "lon"), P(None, "lat", "lon"), P(), P()),
        check_vma=False,
    )
```

```python
import functools

import jax
import jax.numpy as jnp
from jax import lax
from jax.experimental import pallas as pl
from jax.experimental.pallas import tpu as pltpu
from jax.sharding import PartitionSpec as P

MESH = pl.DeviceIdType.MESH
LINK = jnp.bfloat16
F32 = jnp.float32
BF16 = jnp.bfloat16


def dot(left, right, dims):
    return lax.dot_general(left, right, (dims, ((), ())), preferred_element_type=F32)


def shifted(value, amount):
    return pltpu.roll(value, amount, 1)


def pack_columns(load, out_ref, count, group, tall, width):
    lane = lax.broadcasted_iota(jnp.int32, (group, width), 1)
    for start in range(0, count, group):
        first = jnp.zeros((group, width), F32)
        last = jnp.zeros((group, width), F32)
        for row in range(tall):
            cells = load(row, start, group).astype(F32)
            first = jnp.where(lane == row, shifted(cells, row) if row else cells, first)
            last = jnp.where(lane == row, shifted(cells, row + 1), last)
        out_ref[0, start : start + group] = first.astype(BF16)
        out_ref[1, start : start + group] = last.astype(BF16)


def widen_row(load, halo_ref, row, start, group, width):
    lane = lax.broadcasted_iota(jnp.int32, (group, width), 1)
    cells = load(row, start, group)
    wide = cells.astype(F32)
    left = shifted(halo_ref[0, start : start + group].astype(F32), lax.rem(width - row, width))
    right = shifted(halo_ref[1, start : start + group].astype(F32), width - 1 - row)
    before = jnp.where(lane == 0, left, shifted(wide, 1)).astype(BF16)
    after = jnp.where(lane == width - 1, right, shifted(wide, width - 1)).astype(BF16)
    return before, cells, after


def padded_loader(inner, halo, height):
    def load(row, start, group):
        if isinstance(row, int) and row in (0, height + 1):
            return halo[min(row, 1), start : start + group]
        return inner[row - 1, start : start + group]

    return load


def layer_kernel(
    lats, halves, deep, wide_deep, in_ref, we_ref, wf_ref, wr_ref, reb_ref, feat_ref, grad_ref,
    xg, hs, hrow, pre, hidhalo, packed, arrived, hpacked, harrived, accx, accg, parts,
    from_pair, lon_out, from_lon, lat_out, from_lat, *sems,
):
    height, both, width = in_ref.shape
    hid = hrow.shape[1]
    lons = 2 * halves
    band = 3 * wide_deep
    lat = lax.axis_index("lat")
    lon = lax.axis_index("lon")
    half = lax.div(lon, 2)
    core = lax.rem(lon, 2)
    other = 1 - core
    below_top = lax.div(lat + lats - 1, lats)
    above_end = lax.div(2 * lats - 2 - lat, lats)

    def lon_peer(step):
        return (lat, lax.rem(half + step, halves) * 2 + core)

    def lat_peer(step):
        return (lax.rem(lat + step, lats), lon)

    pair = (lat, half * 2 + other)
    outer = (lat, lax.rem(lon + lons + 2 * core - 1, lons))
    west = (lat, lax.rem(lon + lons - 1, lons))
    east = (lat, lax.rem(lon + 1, lons))
    north = (lat - below_top, lax.rem(lon + (1 - below_top) * halves, lons))
    south = (lat + above_end, lax.rem(lon + (1 - above_end) * halves, lons))

    barrier = pltpu.get_barrier_semaphore()
    peers = [pair, outer]
    peers += [lon_peer(step) for step in range(1, halves)]
    peers += [lat_peer(step) for step in range(1, lats)]
    for peer in peers:
        pl.semaphore_signal(barrier, inc=1, device_id=peer, device_id_type=MESH)

    def send(src, dst, phase, send_slot, recv_slot, peer):
        copy = pltpu.make_async_remote_copy(
            src_ref=src,
            dst_ref=dst,
            send_sem=sems[2 * phase].at[send_slot],
            recv_sem=sems[2 * phase + 1].at[recv_slot],
            device_id=peer,
            device_id_type=MESH,
        )
        copy.start()
        return copy

    def swap_columns(source, target, phase):
        return [
            send(source.at[1], target.at[0], phase, 0, 0, east),
            send(source.at[0], target.at[1], phase, 1, 1, west),
        ]

    def swap_rows(rows, halo, phase):
        return [
            send(rows.at[0], halo.at[below_top], phase, 0, below_top, north),
            send(rows.at[height - 1], halo.at[1 - above_end], phase, 1, 1 - above_end, south),
        ]

    def wait_rows(copies, halo, phase):
        for copy in copies:
            copy.wait_send()
        for slot in range(2):
            edge = halo.at[slot]
            pltpu.make_async_copy(edge, edge, sems[2 * phase + 1].at[slot]).wait()

    def load_in(row, start, group):
        return in_ref[row, start : start + group]

    load_hid = padded_loader(hrow, hidhalo, height)
    pack_columns(load_in, packed, both, both // 2, height, width)
    pl.semaphore_wait(barrier, len(peers))
    copies = swap_columns(packed, arrived, 12)
    accx[...] = jnp.zeros_like(accx)
    accg[...] = jnp.zeros_like(accg)
    for copy in copies:
        copy.wait()

    def widen_in(row):
        before, cells, after = widen_row(load_in, arrived, row, 0, wide_deep, width)
        for place, value in enumerate((before, cells, after)):
            xg[row + 1, place * wide_deep : (place + 1) * wide_deep] = value
        before, cells, after = widen_row(load_in, arrived, row, wide_deep, wide_deep, width)
        for place, value in enumerate((after, cells, before)):
            xg[row + 1, band + place * wide_deep : band + (place + 1) * wide_deep] = value

    widen_in(0)
    widen_in(height - 1)
    copies = [
        send(xg.at[1], xg.at[below_top * (height + 1)], 13, 0, below_top, north),
        send(xg.at[height], xg.at[(1 - above_end) * (height + 1)], 13, 1, 1 - above_end, south),
    ]

    @pl.loop(1, height - 1)
    def _(row):
        widen_in(row)

    def window(ref, row, start, count):
        return jnp.concatenate(
            [
                ref[pl.ds(row + place, 3), start : start + count].reshape(3 * count, width)
                for place in range(rows)
            ],
            axis=1,
        )

    def first_step(step):
        row = step * rows
        in_cols = window(xg, row, 0, band)
        cot_cols = window(xg, row, band, band)
        pre_act = dot(we_ref[...], in_cols, ((1,), (0,)))
        pre[step] = pre_act
        hidden = (pre_act * (1.0 / (1.0 + jnp.exp(-pre_act)))).astype(BF16)
        for place in range(rows):
            hrow[row + place] = hidden[:, place * width : (place + 1) * width]
        accg[...] += dot(cot_cols, hidden, ((1,), (1,)))

    def second_step(step, extra):
        row = step * rows
        in_cols = window(xg, row, 0, band)
        cot_cols = window(xg, row, band, band)
        pre_act = pre[step]
        logistic = 1.0 / (1.0 + jnp.exp(-pre_act))
        feat = dot(wf_ref[...], cot_cols, ((1,), (0,)))
        if extra is not None:
            feat = feat + extra
        feat = feat.astype(BF16)
        for place in range(rows):
            feat_ref[row + place] = feat[:, place * width : (place + 1) * width]
        pre_grad = (
            feat.astype(F32) * logistic * (1.0 + pre_act * (1.0 - logistic))
        ).astype(BF16)
        accx[...] += dot(in_cols, pre_grad, ((1,), (1,)))

    rows = 4
    steps = height // rows
    ends = ((0, below_top, 2 * band, 0), (1, above_end, 0, height - 1))

    @pl.loop(1, steps - 1)
    def _(step):
        first_step(step)

    for copy in copies:
        copy.wait_send()
    for slot in range(2):
        edge = xg.at[slot * (height + 1)]
        pltpu.make_async_copy(edge, edge, sems[27].at[slot]).wait()
    at_poles = []
    for slot, inside, start, row in ends:
        edge = xg[slot * (height + 1), band:]
        at_poles.append(jnp.where(inside == 0, edge, jnp.zeros_like(edge)))
        xg[slot * (height + 1), band:] = jnp.where(inside == 0, jnp.zeros_like(edge), edge)
    first_step(0)
    first_step(steps - 1)
    row_copies = swap_rows(hrow, hidhalo, 15)
    for slot, inside, start, row in ends:
        accg[start : start + band] += dot(at_poles[slot], hrow[row], ((1,), (1,)))

    lane = hid // 2
    lane_rows = parts.shape[2]
    lon_rows = lane_rows // halves
    lat_rows = lon_rows // lats

    def fill(stream, acc, backward):
        for tap in range(9):
            row_tap, col_tap = divmod(tap, 3)
            source = ((2 - row_tap) * 3 + col_tap if backward else tap) * wide_deep
            for side in range(2):
                parts[stream, side, tap * deep : (tap + 1) * deep] = acc[
                    source : source + deep, side * lane : (side + 1) * lane
                ]
        used = 9 * deep
        if lane_rows > used:
            for side in range(2):
                parts[stream, side, used:] = jnp.zeros((lane_rows - used, lane), F32)

    def piece(index, count):
        return pl.ds(pl.multiple_of(index * count, 16), count)

    order = sorted(range(1, lats), key=lambda step: abs(2 * step - lats))

    def start_pair(stream):
        copies = {}
        for step in list(range(1, halves)) + [0]:
            part = piece(lax.rem(half + step, halves), lon_rows)
            copies[step] = send(
                parts.at[stream, other, part], from_pair.at[stream, part], stream * 6, step, step, pair
            )
        return copies

    def start_lon(stream, copies):
        onward = {}
        for step in range(1, halves):
            copies[step].wait()
            target = lax.rem(half + step, halves)
            part = piece(target, lon_rows)
            lon_out[stream, part] = (parts[stream, core, part] + from_pair[stream, part]).astype(LINK)
            for turn in order + [0]:
                there = lax.rem(lat + turn, lats)
                onward[step, turn] = send(
                    lon_out.at[stream, piece(target * lats + there, lat_rows)],
                    from_lon.at[stream, step - 1, piece(there, lat_rows)],
                    stream * 6 + 1, (step - 1) * lats + turn, (step - 1) * lats + turn, lon_peer(step),
                )
        copies[0].wait()
        return onward

    def lon_total(stream, copies, turn):
        there = lax.rem(lat + turn, lats)
        part = piece(half * lats + there, lat_rows)
        total = parts[stream, core, part] + from_pair[stream, part]
        for step in range(1, halves):
            copies[step, turn].wait()
            total = total + from_lon[stream, step - 1, piece(there, lat_rows)].astype(F32)
        return total

    def start_lat(stream, copies):
        onward = []
        for turn in order:
            there = piece(lax.rem(lat + turn, lats), lat_rows)
            lat_out[stream, there] = lon_total(stream, copies, turn).astype(LINK)
            onward.append(
                send(
                    lat_out.at[stream, there], from_lat.at[stream, turn - 1],
                    stream * 6 + 2, turn - 1, turn - 1, lat_peer(turn),
                )
            )
        return onward, lon_total(stream, copies, 0)

    def spread(stream, turn, lon_copies, pair_copies):
        there = lax.rem(lat + lats - turn, lats)
        mine = grad_ref.at[stream, core, piece(half * lats + there, lat_rows)]
        for step in range(1, halves):
            slot = (step - 1) * lats + turn
            lon_copies[step, turn] = send(mine, mine, stream * 6 + 4, slot, slot, lon_peer(step))
        pair_copies.append(send(mine, mine, stream * 6 + 5, turn, turn, pair))

    def start_lat_gather(stream, started):
        copies, total = started
        for turn, copy in zip(order, copies):
            copy.wait()
            total = total + from_lat[stream, turn - 1].astype(F32)
        place = piece(half * lats + lat, lat_rows)
        grad_ref[stream, core, place] = total.astype(grad_ref.dtype)
        mine = grad_ref.at[stream, core, place]
        copies = [
            send(mine, mine, stream * 6 + 3, turn - 1, turn - 1, lat_peer(turn)) for turn in order
        ]
        lon_copies, pair_copies = {}, []
        spread(stream, 0, lon_copies, pair_copies)
        return copies, lon_copies, pair_copies

    def start_spread(stream, started):
        copies, lon_copies, pair_copies = started
        for turn, copy in reversed(list(zip(order, copies))):
            copy.wait()
            spread(stream, turn, lon_copies, pair_copies)
        return lon_copies, pair_copies

    def start_pair_gather(stream, started):
        lon_copies, pair_copies = started
        for turn in [0] + order[::-1]:
            for step in range(1, halves):
                lon_copies[step, turn].wait()
                source = lax.rem(half + halves - step, halves)
                there = lax.rem(lat + lats - turn, lats)
                mine = grad_ref.at[stream, core, piece(source * lats + there, lat_rows)]
                slot = step * lats + turn
                pair_copies.append(send(mine, mine, stream * 6 + 5, slot, slot, pair))
        return pair_copies

    fill(0, accg, True)
    gen_copies = start_pair(0)

    @pl.loop(1, steps - 1)
    def _(step):
        second_step(step, None)

    gen_copies = start_lon(0, gen_copies)
    open_gap = jnp.zeros((hid, (rows - 1) * width), F32)
    for slot, inside, start, row in ends:
        term = dot(wf_ref[:, start : start + band], at_poles[slot], ((1,), (0,)))
        both_terms = [term, open_gap] if slot == 0 else [open_gap, term]
        second_step(row // rows, jnp.concatenate(both_terms, axis=1))
    fill(1, accx, False)
    enc_copies = start_pair(1)
    gen_copies = start_lat(0, gen_copies)
    enc_copies = start_lon(1, enc_copies)
    wait_rows(row_copies, hidhalo, 15)
    pack_columns(load_hid, hpacked, hid, 64, height + 2, width)
    column_copies = swap_columns(hpacked, harrived, 14)
    enc_copies = start_lat(1, enc_copies)
    gen_copies = start_lat_gather(0, gen_copies)
    for copy in column_copies:
        copy.wait()

    def widen_hid(row):
        for start in range(0, hid, 64):
            parts_row = widen_row(load_hid, harrived, row, start, 64, width)
            for place, value in enumerate(parts_row):
                hs[row, place * hid + start : place * hid + start + 64] = value

    widen_hid(0)
    widen_hid(height + 1)

    @pl.loop(1, height + 1)
    def _(row):
        widen_hid(row)

    enc_copies = start_lat_gather(1, enc_copies)
    gen_copies = start_spread(0, gen_copies)

    @pl.loop(0, steps)
    def _(step):
        value = dot(wr_ref[...], window(hs, step * rows, 0, 3 * hid), ((1,), (0,))).astype(BF16)
        for place in range(rows):
            reb_ref[step * rows + place] = value[:, place * width : (place + 1) * width]

    gen_copies = start_pair_gather(0, gen_copies)
    enc_copies = start_spread(1, enc_copies)
    enc_copies = start_pair_gather(1, enc_copies)
    for copy in gen_copies + enc_copies:
        copy.wait()


def on_device(fields, enc_kernel, gen_kernel, recon_grad):
    in_count, height, width = fields.shape
    hid = enc_kernel.shape[2]
    deep = -(-in_count // 8) * 8
    wide_deep = -(-in_count // 16) * 16
    extra = wide_deep - in_count
    lats = lax.axis_size("lat")
    lons = lax.axis_size("lon")
    halves = lons // 2
    room = ((0, 0), (0, extra), (0, 0))
    stacked = jnp.concatenate(
        [
            jnp.pad(fields.transpose(1, 0, 2), room),
            jnp.pad(recon_grad.transpose(1, 0, 2), room),
        ],
        axis=1,
    )
    band = 3 * wide_deep
    enc_flat = jnp.pad(enc_kernel, ((0, 0), (0, 0), (0, 0), (0, extra)))
    enc_flat = enc_flat.transpose(2, 0, 1, 3).reshape(hid, 3 * band)
    gen_taps = jnp.pad(gen_kernel, ((0, 0), (0, 0), (0, extra), (0, 0)))
    back_flat = gen_taps[::-1].transpose(3, 0, 1, 2).reshape(hid, 3 * band)
    gen_flat = gen_taps.transpose(2, 0, 1, 3).reshape(wide_deep, 9 * hid)
    lane = hid // 2
    lat_rows = -(-9 * deep // (halves * lats * 16)) * 16
    lon_rows = lats * lat_rows
    lane_rows = halves * lon_rows
    hops = (halves - 1) * lats
    counts = [halves, hops, lats - 1, lats - 1, hops, halves * lats] * 2 + [2] * 4
    rebuilt, feat, summed = pl.pallas_call(
        functools.partial(layer_kernel, lats, halves, deep, wide_deep),
        out_shape=[
            jax.ShapeDtypeStruct((height, wide_deep, width), BF16),
            jax.ShapeDtypeStruct((height, hid, width), BF16),
            jax.ShapeDtypeStruct((2, 2, lane_rows, lane), BF16),
        ],
        in_specs=[pl.BlockSpec(memory_space=pltpu.VMEM)] * 4,
        out_specs=[pl.BlockSpec(memory_space=pltpu.VMEM)] * 3,
        scratch_shapes=[
            pltpu.VMEM((height + 2, 2 * band, width), BF16),
            pltpu.VMEM((height + 2, 3 * hid, width), BF16),
            pltpu.VMEM((height, hid, width), BF16),
            pltpu.VMEM((height // 4, hid, 4 * width), F32),
            pltpu.VMEM((2, hid, width), BF16),
            pltpu.VMEM((2, 2 * wide_deep, width), BF16),
            pltpu.VMEM((2, 2 * wide_deep, width), BF16),
            pltpu.VMEM((2, hid, width), BF16),
            pltpu.VMEM((2, hid, width), BF16),
            pltpu.VMEM((3 * band, hid), F32),
            pltpu.VMEM((3 * band, hid), F32),
            pltpu.VMEM((2, 2, lane_rows, lane), F32),
            pltpu.VMEM((2, lane_rows, lane), F32),
            pltpu.VMEM((2, lane_rows, lane), LINK),
            pltpu.VMEM((2, halves - 1, lon_rows, lane), LINK),
            pltpu.VMEM((2, lon_rows, lane), LINK),
            pltpu.VMEM((2, lats - 1, lat_rows, lane), LINK),
        ]
        + [pltpu.SemaphoreType.DMA((count,)) for count in counts for _ in range(2)],
        compiler_params=pltpu.CompilerParams(
            collective_id=0, has_side_effects=True, vmem_limit_bytes=48 << 20
        ),
    )(stacked, enc_flat, back_flat, gen_flat)
    norm_scale = 1.0 / jnp.sqrt(F32(height * lats * width * lons))
    grads = jnp.concatenate([summed[:, 0, : 9 * deep], summed[:, 1, : 9 * deep]], axis=2)
    grads = grads.reshape(2, 3, 3, deep, hid)[:, :, :, :in_count].astype(F32) * norm_scale
    return (
        rebuilt[:, :in_count].transpose(1, 0, 2),
        feat.transpose(1, 0, 2),
        grads[1].transpose(0, 1, 3, 2),
        grads[0],
    )


def solution(mesh):
    return jax.shard_map(
        on_device,
        mesh=mesh,
        in_specs=(P(None, "lat", "lon"), P(), P(), P(None, "lat", "lon")),
        out_specs=(P(None, "lat", "lon"), P(None, "lat", "lon"), P(), P()),
        check_vma=False,
    )
```
